32 devices in a mesh: dp: 8 (over y, x, core), mp: 4 (over z).
Axes of the slice: x: 2, y: 2, z: 4, core: 2. Of those that a mesh axis runs over, the one named last changes fastest.
Arguments:
- queries: bfloat16 [2048, 2048], P('dp', 'mp'), may hold values from -24 to 24
- context_grad: bfloat16 [2048, 2048], P('dp', 'mp'), may hold values from -6 to 6
- encoder_rows: bfloat16 [7168, 4096], P('dp'), may hold values from -60 to 60
- key_weight: bfloat16 [4096, 2048], P('dp', 'mp'), may hold values from -1 to 1
- value_weight: bfloat16 [4096, 2048], P('dp', 'mp'), may hold values from -0.09375 to 0.09375
- document_lengths: int32 [8, 4], P('dp'), may hold values from 1 to 128, 256 in all within a row
- block_bin: int32 [56], P('dp'), may hold values from 0 to 7, as said below
- block_document: int32 [56], P('dp'), may hold values from 0 to 3
Outputs:
- context: bfloat16 [2048, 2048], P('dp', 'mp')
- query_grad: bfloat16 [2048, 2048], P('dp', 'mp')
- encoder_grad: bfloat16 [7168, 4096], P('dp', 'mp')
- key_weight_grad: bfloat16 [4096, 2048], P('dp', 'mp')
- value_weight_grad: bfloat16 [4096, 2048], P('dp', 'mp')
The draws below stay inside these ranges and needn't reach their ends.
Inputs may be any that keep to these rules, and one draw needn't show every extreme that they name: `block_bin`: each index of dp holds 7 encoder blocks and sends them to 7 different bins; one bin receives a block from every index of dp.
All inputs are finite; a program needn't handle non-finite values.
Results may differ from the reference program's by a relative error of at most 0.03.
The reference program's roundings to bfloat16 on the way count: a program that leaves them out, or rounds other values in their place, can miss the bound.
Values may be sent and summed in bfloat16 or wider, within the bound.
A program may use at most 128 MiB of HBM per device.

```python
import math
import jax
import jax.numpy as jnp
import numpy as np
from jax import lax

D = 4096
HD = 256
H = 8
BLK = 128
NDOC = 4
EBLK = 7
DEC_DEV = 256
ENC_DEV = 896
TOKENS = 2048
ENC_ROWS = 7168
NBLK = 56
N_DP = 8


def draw_queries(key, part):
    values = jnp.clip(jax.random.normal(jax.random.fold_in(key, 11), (TOKENS, H * HD), jnp.float32), -6.0, 6.0)
    return values.astype(jnp.bfloat16)


def draw_encoder_rows(key, part):
    bin_count = ENC_ROWS // ENC_DEV
    slice_width = D // bin_count
    pairing = jax.random.permutation(jax.random.fold_in(key, 21), bin_count)
    owner = jnp.arange(ENC_ROWS, dtype=jnp.int32) // ENC_DEV
    feature_block = jnp.arange(D, dtype=jnp.int32) // slice_width
    boost = jnp.where(pairing[owner][:, None] == feature_block[None, :], 3.0, 1.0)
    values = jax.random.normal(jax.random.fold_in(key, 24), (ENC_ROWS, D), jnp.float32)
    return jnp.clip(values * boost, -60.0, 60.0).astype(jnp.bfloat16)


def draw_key_weight(key, part):
    noise = jax.random.normal(jax.random.fold_in(key, 31), (D, H * HD), jnp.float32) * D ** (-0.5)
    values = noise
    return jnp.clip(values, -1.0, 1.0).astype(jnp.bfloat16)


def draw_block_bin(key, part):
    bin_count = NBLK // EBLK
    heavy = jax.random.randint(jax.random.fold_in(key, 41), (), 0, bin_count)
    leaning = jax.random.randint(jax.random.fold_in(key, 42), (bin_count,), 0, 4)
    jitter = jax.random.randint(jax.random.fold_in(key, 43), (bin_count, bin_count), 0, 1024)
    columns = jnp.arange(bin_count, dtype=jnp.int32)
    ranking = leaning[None, :] * 2 ** 20 + jitter * 64 + columns[None, :]
    ranking = jnp.where(columns[None, :] == heavy, 2 ** 29, ranking).astype(jnp.int32)
    _, chosen = lax.top_k(ranking, EBLK)
    shuffle_keys = jax.random.randint(jax.random.fold_in(key, 44), (bin_count, EBLK), 0, 1024) * 64 + jnp.arange(EBLK, dtype=jnp.int32)[None, :]
    order = jnp.argsort(shuffle_keys, axis=1)
    chosen = jnp.take_along_axis(chosen, order, axis=1)
    return chosen.reshape(-1).astype(jnp.int32)


def with_ends(values, key, least, top_value):
    place = [jax.random.randint(jax.random.fold_in(key, axis), (), 0, length) for axis, length in enumerate(values.shape)]
    widest = values.shape.index(max(values.shape))
    beside = place[:widest] + [(place[widest] + 1) % values.shape[widest]] + place[widest + 1:]
    return values.at[tuple(place)].set(least).at[tuple(beside)].set(top_value)


def block_scale(stream_key, shape, pieces, least, largest):
    level = 1.0
    for position, parts in pieces:
        steps = jax.random.uniform(jax.random.fold_in(jax.random.fold_in(stream_key, 6), position), (parts,), jnp.float32, least / len(pieces), largest / len(pieces))
        level = level * jnp.repeat(jnp.exp(steps), shape[position] // parts).reshape((-1,) + (1,) * (len(shape) - 1 - position))
    return level


def split_up(count, total, most, skew):
    loads = [(1 << 20) // math.isqrt(rank ** skew) + 1 for rank in range(2, count + 1)]
    spare, holding = total - most - (count - 1), [1] * (count - 1)
    while spare > 0:
        candidates = [i for i in range(count - 1) if holding[i] < most]
        pool, remaining = sum([loads[i] for i in candidates]), spare
        for i in candidates:
            extra = min(most - holding[i], max(1, remaining * loads[i] // pool), spare)
            holding[i] = holding[i] + extra
            spare = spare - extra
    return np.array([most] + holding)


def uneven(own_key, number_of, total, limit, skew):
    if number_of == 2:
        one = jax.random.randint(own_key, (), max(1, total - limit), min(limit, total - 1) + 1)
        return jnp.stack([one, total - one])
    lengths = jnp.asarray(split_up(number_of, total, limit, skew), jnp.int32)
    couples = (number_of - 1) // 2
    source_of, taker = lengths[1:1 + 2 * couples:2], lengths[2:2 + 2 * couples:2]
    margin = jnp.minimum(source_of - 1, limit - taker)
    shifted = jax.random.randint(jax.random.fold_in(own_key, 1), (couples,), 0, 1 << 20) % (margin + 1)
    lengths = lengths.at[1:1 + 2 * couples:2].set(source_of - shifted).at[2:2 + 2 * couples:2].set(taker + shifted)
    return lengths[jax.random.permutation(jax.random.fold_in(own_key, 2), number_of)]


def normal_values(key, shape, spread, limit, shards=(), kind=jnp.bfloat16):
    loudness = block_scale(key, shape, shards, -0.22, 0.18) if shards else 1.0
    result = jax.random.normal(key, shape, jnp.float32) * spread * loudness
    return jnp.minimum(jnp.maximum(result, -limit), limit).astype(kind)


def setup_inputs(seed: int = 0) -> dict:
    key_list = jax.random.split(jax.random.key(seed), 9)
    return {
        "queries": draw_queries(jax.random.fold_in(key_list[8], 71), 0),
        "context_grad": normal_values(key_list[1], (TOKENS, H * HD), 1.0, 6.0, ((0, 8), (1, 4))),
        "encoder_rows": draw_encoder_rows(jax.random.fold_in(key_list[8], 71), 0),
        "key_weight": draw_key_weight(jax.random.fold_in(key_list[8], 71), 0),
        "value_weight": normal_values(key_list[4], (D, H * HD), D ** -0.5, 0.09375, ((0, 8), (1, 4))),
        "document_lengths": jax.vmap(lambda own: uneven(own, NDOC, DEC_DEV, DEC_DEV // 2, 2))(jax.random.split(key_list[5], N_DP)).reshape((N_DP, NDOC)).astype(jnp.int32),
        "block_bin": draw_block_bin(jax.random.fold_in(key_list[8], 71), 0),
        "block_document": with_ends(jax.random.randint(key_list[7], (NBLK,), 0, NDOC), jax.random.fold_in(key_list[7], 1), 0, NDOC - 1).astype(jnp.int32),
    }


masked_value = -1e30


def attend_weights(scores, live_mask):
    present = jnp.any(live_mask, axis=1)[None, :, None]
    blocked = jnp.where(live_mask[None], scores, masked_value)
    highest = jnp.max(blocked, axis=2, keepdims=True)
    highest = jnp.where(present, highest, 0.0)
    raised = jnp.exp(jnp.where(live_mask[None], scores - highest, masked_value))
    totals = jnp.maximum(jnp.sum(raised, axis=2, keepdims=True), 1.0)
    return raised / totals


def reference(queries, context_grad, encoder_rows, key_weight, value_weight, document_lengths, block_bin, block_document):
    width = H * HD
    scaling = HD ** -0.5
    both_weights = jnp.concatenate([key_weight, value_weight], axis=1).astype(jnp.float32)
    key_values = jnp.dot(encoder_rows.astype(jnp.float32), both_weights).astype(jnp.bfloat16)
    kv_blocks = key_values.reshape(N_DP, EBLK, BLK, 2 * width)
    bins_of = block_bin.reshape(N_DP, EBLK)
    docs_of = block_document.reshape(N_DP, EBLK)
    sources = jnp.arange(N_DP, dtype=jnp.int32)
    local_slots = jnp.arange(EBLK, dtype=jnp.int32)
    positions = jnp.arange(DEC_DEV, dtype=jnp.int32)

    def bin_step(grad_blocks, bin_index):
        arrives = bins_of == bin_index
        present = jnp.any(arrives, axis=1)
        local_index = jnp.sum(jnp.where(arrives, local_slots[None, :], 0), axis=1).astype(jnp.int32)
        slot_kv = kv_blocks[sources, local_index]
        slot_doc = jnp.where(present, docs_of[sources, local_index], -1)
        doc_ends = jnp.cumsum(document_lengths[bin_index])
        token_doc = jnp.sum((doc_ends[None, :] <= positions[:, None]).astype(jnp.int32), axis=1)
        live_mask = token_doc[:, None] == jnp.repeat(slot_doc, BLK)[None, :]
        key_rows = slot_kv[:, :, :width].reshape(N_DP * BLK, H, HD).astype(jnp.float32)
        value_rows = slot_kv[:, :, width:].reshape(N_DP * BLK, H, HD).astype(jnp.float32)
        row_start = (bin_index * DEC_DEV).astype(jnp.int32)
        query_rows = lax.dynamic_slice_in_dim(queries, row_start, DEC_DEV, 0).reshape(DEC_DEV, H, HD).astype(jnp.float32)
        grad_rows = lax.dynamic_slice_in_dim(context_grad, row_start, DEC_DEV, 0).reshape(DEC_DEV, H, HD).astype(jnp.float32)
        scores = jnp.einsum("thd,shd->hts", query_rows, key_rows) * scaling
        attention = attend_weights(scores, live_mask)
        rounded = lax.optimization_barrier(attention.astype(jnp.bfloat16)).astype(jnp.float32)
        context = jnp.einsum("hts,shd->thd", rounded, value_rows).astype(jnp.bfloat16)
        grad_raw = jnp.einsum("thd,shd->hts", grad_rows, value_rows)
        deltas = jnp.sum(attention * grad_raw, axis=2, keepdims=True)
        score_grad = lax.optimization_barrier((attention * (grad_raw - deltas) * scaling).astype(jnp.bfloat16)).astype(jnp.float32)
        query_grad = jnp.einsum("hts,shd->thd", score_grad, key_rows).astype(jnp.bfloat16)
        key_grad = jnp.einsum("hts,thd->shd", score_grad, query_rows).astype(jnp.bfloat16)
        value_grad = jnp.einsum("hts,thd->shd", rounded, grad_rows).astype(jnp.bfloat16)
        slot_grads = jnp.concatenate([key_grad.reshape(N_DP, BLK, width), value_grad.reshape(N_DP, BLK, width)], axis=2)
        grad_blocks = jnp.where(arrives[:, :, None, None], slot_grads[:, None], grad_blocks)
        return grad_blocks, (context.reshape(DEC_DEV, width), query_grad.reshape(DEC_DEV, width))

    start_blocks = jnp.zeros((N_DP, EBLK, BLK, 2 * width), jnp.bfloat16)
    grad_blocks, (context_all, query_all) = lax.scan(bin_step, start_blocks, jnp.arange(N_DP, dtype=jnp.int32))
    context = context_all.reshape(TOKENS, width)
    query_grad = query_all.reshape(TOKENS, width)
    kv_grad = grad_blocks.reshape(N_DP, ENC_DEV, 2 * width)
    encoder_split = encoder_rows.reshape(N_DP, ENC_DEV, D)

    def add_source(weight_sum, source):
        partial_value = jnp.dot(encoder_split[source].astype(jnp.float32).T, kv_grad[source].astype(jnp.float32))
        partial_value = lax.optimization_barrier(partial_value.astype(jnp.bfloat16)).astype(jnp.float32)
        return weight_sum + partial_value, None

    weight_sum, _ = lax.scan(add_source, jnp.zeros((D, 2 * width), jnp.float32), jnp.arange(N_DP, dtype=jnp.int32))
    key_weight_grad = weight_sum[:, :width].astype(jnp.bfloat16)
    value_weight_grad = weight_sum[:, width:].astype(jnp.bfloat16)
    encoder_grad = jnp.dot(kv_grad.reshape(ENC_ROWS, 2 * width).astype(jnp.float32), both_weights.T).astype(jnp.bfloat16)
    return (context, query_grad, encoder_grad, key_weight_grad, value_weight_grad)
```

```python
import functools

import jax
import jax.numpy as jnp
from jax import lax
from jax.experimental import pallas as pl
from jax.experimental.pallas import tpu as pltpu
from jax.sharding import PartitionSpec as P

HD = 256
BLK = 128


masked_value = -1e30


def attend_weights(scores, live_mask):
    present = jnp.any(live_mask, axis=1)[None, :, None]
    blocked = jnp.where(live_mask[None], scores, masked_value)
    highest = jnp.max(blocked, axis=2, keepdims=True)
    highest = jnp.where(present, highest, 0.0)
    raised = jnp.exp(jnp.where(live_mask[None], scores - highest, masked_value))
    totals = jnp.maximum(jnp.sum(raised, axis=2, keepdims=True), 1.0)
    return raised / totals


def token_documents(lengths, token_count):
    doc_ends = jnp.cumsum(lengths)
    positions = jnp.arange(token_count, dtype=jnp.int32)
    return jnp.sum((doc_ends[None, :] <= positions[:, None]).astype(jnp.int32), axis=1)


def per_device(
    queries,
    context_grad,
    encoder_rows,
    key_weight,
    value_weight,
    document_lengths,
    block_bin,
    block_document,
):
    bin_count = lax.axis_size("dp")
    full_key, full_value = (
        lax.all_gather(key_weight, "dp", axis=0, tiled=True),
        lax.all_gather(value_weight, "dp", axis=0, tiled=True),
    )
    head_width = full_key.shape[1]
    head_count = head_width // HD
    block_rows = BLK
    blocks_here = block_bin.shape[0]
    both_weights = jnp.concatenate([full_key, full_value], axis=1)
    projected = jnp.dot(encoder_rows, both_weights, preferred_element_type=jnp.float32).astype(
        jnp.bfloat16
    )
    route_table = (block_bin[:, None] == jnp.arange(bin_count, dtype=jnp.int32)[None, :]).astype(
        jnp.bfloat16
    )
    flat_blocks = projected.reshape(blocks_here, block_rows * 2 * head_width)
    outbound = lax.dot_general(
        route_table, flat_blocks, (((0,), (0,)), ((), ())), preferred_element_type=jnp.float32
    )
    outbound = outbound.astype(jnp.bfloat16).reshape(bin_count, block_rows, 2 * head_width)
    slot_docs = (
        lax.dot_general(
            route_table.astype(jnp.float32),
            (block_document + 1).astype(jnp.float32),
            (((0,), (0,)), ((), ())),
        )
        - 1.0
    )
    tag_rows = jnp.broadcast_to(slot_docs[:, None], (bin_count, block_rows)).astype(jnp.bfloat16)
    arrived, arrived_tags = (
        lax.all_to_all(outbound, "dp", split_axis=0, concat_axis=0, tiled=True),
        lax.all_to_all(tag_rows, "dp", split_axis=0, concat_axis=0, tiled=True),
    )
    key_slots = arrived[:, :, :head_width].reshape(bin_count * block_rows, head_count, HD)
    value_slots = arrived[:, :, head_width:].reshape(bin_count * block_rows, head_count, HD)
    token_count = queries.shape[0]
    token_docs = token_documents(document_lengths[0], token_count).astype(jnp.float32)
    live_mask = arrived_tags.reshape(-1).astype(jnp.float32)[None, :] == token_docs[:, None]
    query_heads = queries.reshape(token_count, head_count, HD)
    grad_heads = context_grad.reshape(token_count, head_count, HD)
    scaling = HD ** (-0.5)
    scores = (
        jnp.einsum("thd,shd->hts", query_heads, key_slots, preferred_element_type=jnp.float32)
        * scaling
    )
    attention = attend_weights(scores, live_mask)
    rounded = attention.astype(jnp.bfloat16)
    context = jnp.einsum(
        "hts,shd->thd", rounded, value_slots, preferred_element_type=jnp.float32
    ).astype(jnp.bfloat16)
    grad_raw = jnp.einsum(
        "thd,shd->hts", grad_heads, value_slots, preferred_element_type=jnp.float32
    )
    deltas = jnp.sum(attention * grad_raw, axis=2, keepdims=True)
    score_grad = (attention * (grad_raw - deltas) * scaling).astype(jnp.bfloat16)
    query_grad = jnp.einsum(
        "hts,shd->thd", score_grad, key_slots, preferred_element_type=jnp.float32
    ).astype(jnp.bfloat16)
    key_grad = jnp.einsum(
        "hts,thd->shd", score_grad, query_heads, preferred_element_type=jnp.float32
    ).astype(jnp.bfloat16)
    value_grad = jnp.einsum(
        "hts,thd->shd", rounded, grad_heads, preferred_element_type=jnp.float32
    ).astype(jnp.bfloat16)
    slot_grads = jnp.concatenate(
        [
            key_grad.reshape(bin_count, block_rows, head_width),
            value_grad.reshape(bin_count, block_rows, head_width),
        ],
        axis=2,
    )
    returned = lax.all_to_all(slot_grads, "dp", split_axis=0, concat_axis=0, tiled=True)
    own_grads = jnp.dot(
        route_table,
        returned.reshape(bin_count, block_rows * 2 * head_width),
        preferred_element_type=jnp.float32,
    )
    own_grads = own_grads.astype(jnp.bfloat16).reshape(encoder_rows.shape[0], 2 * head_width)
    weight_terms = lax.dot_general(
        encoder_rows, own_grads, (((0,), (0,)), ((), ())), preferred_element_type=jnp.float32
    )
    weight_sums = lax.psum_scatter(
        weight_terms.astype(jnp.bfloat16), "dp", scatter_dimension=0, tiled=True
    ).astype(jnp.float32)
    key_weight_grad = weight_sums[:, :head_width].astype(jnp.bfloat16)
    value_weight_grad = weight_sums[:, head_width:].astype(jnp.bfloat16)
    row_terms = lax.dot_general(
        own_grads, both_weights, (((1,), (1,)), ((), ())), preferred_element_type=jnp.float32
    )
    encoder_grad = lax.psum_scatter(
        row_terms.astype(jnp.bfloat16), "mp", scatter_dimension=1, tiled=True
    )
    return (
        context.reshape(token_count, head_width),
        query_grad.reshape(token_count, head_width),
        encoder_grad,
        key_weight_grad,
        value_weight_grad,
    )


MESH = pl.DeviceIdType.MESH


def contract(a, b, dim_a, dim_b):
    return lax.dot_general(
        a, b, (((dim_a,), (dim_b,)), ((), ())), preferred_element_type=jnp.float32
    )


def front_kernel(
    n,
    q_ref,
    g_ref,
    enc_hbm,
    kw_ref,
    vw_ref,
    tags_ref,
    routes_ref,
    token_doc_ref,
    ctx_ref,
    qg_ref,
    back_hbm,
    wfull_hbm,
    enc,
    wts,
    acc,
    outbound,
    arrived,
    arrived_tags,
    grads,
    ret,
    local_sem,
    gather_send,
    gather_recv,
    tag_send,
    tag_recv,
    out_send,
    out_recv,
    back_send,
    back_recv,
):
    me = lax.axis_index("dp")
    core = me % 2
    x = (me // 2) % 2
    y = me // 4

    def place(py, px, pc):
        return (py * 2 + px) * 2 + pc

    at_x, at_y = place(y, 1 - x, core), place(1 - y, x, core)
    at_c, at_d = place(y, x, 1 - core), place(1 - y, 1 - x, core)
    c_x, c_y = place(y, 1 - x, 1 - core), place(1 - y, x, 1 - core)
    c_d = place(1 - y, 1 - x, 1 - core)
    depth, width = kw_ref.shape
    rows = enc.shape[0]
    slots = n
    blk = BLK

    load_enc = pltpu.make_async_copy(enc_hbm, enc, local_sem.at[0])
    load_enc.start()
    barrier = pltpu.get_barrier_semaphore()
    for d in range(1, n):
        pl.semaphore_signal(
            barrier, inc=1, device_id={"dp": (me + d) % n}, device_id_type=MESH
        )
    pl.semaphore_wait(barrier, n - 1)

    def land(src, part):
        return wts.at[src, :, pl.ds(part * width, width)]

    started = []

    def ship(ident, ref, src, part, to):
        copy = pltpu.make_async_remote_copy(
            src_ref=ref,
            dst_ref=land(src, part),
            send_sem=gather_send.at[ident],
            recv_sem=gather_recv.at[ident],
            device_id={"dp": to},
            device_id_type=MESH,
        )
        copy.start()
        started.append(copy)

    def landed(ident, src, part):
        pltpu.make_async_remote_copy(
            src_ref=land(src, part),
            dst_ref=land(src, part),
            send_sem=gather_send.at[ident],
            recv_sem=gather_recv.at[ident],
            device_id={"dp": at_c},
            device_id_type=MESH,
        ).wait_recv()

    ship(0, kw_ref, me, 0, at_x)
    ship(3, vw_ref, me, 1, at_y)
    ship(1, vw_ref, me, 1, at_x)
    ship(2, kw_ref, me, 0, at_y)
    ship(6, kw_ref, me, 0, at_c)
    ship(7, vw_ref, me, 1, at_c)
    own_k = pltpu.make_async_copy(kw_ref, land(me, 0), local_sem.at[1])
    own_v = pltpu.make_async_copy(vw_ref, land(me, 1), local_sem.at[2])
    own_k.start()
    own_v.start()
    tag_copies = []
    for d in range(1, n):
        to = (me + d) % n
        copy = pltpu.make_async_remote_copy(
            src_ref=tags_ref.at[to],
            dst_ref=arrived_tags.at[me],
            send_sem=tag_send.at[d],
            recv_sem=tag_recv.at[d],
            device_id={"dp": to},
            device_id_type=MESH,
        )
        copy.start()
        tag_copies.append(copy)
    arrived_tags[me] = tags_ref[me]
    own_k.wait()
    own_v.wait()
    load_enc.wait()

    tile = rows // 2

    def multiply(src, part, first=False):
        columns = pl.ds(pl.multiple_of(src * depth, depth), depth)
        cols = pl.ds(part * width, width)

        @pl.loop(0, 2)
        def _(t):
            r = pl.ds(pl.multiple_of(t * tile, tile), tile)
            product = jnp.dot(
                enc[r, columns], wts[src, :, cols], preferred_element_type=jnp.float32
            )
            if first:
                acc[r, cols] = product
            else:
                acc[r, cols] += product

    multiply(me, 0, True)
    multiply(me, 1, True)
    landed(6, at_c, 0)
    multiply(at_c, 0)
    landed(7, at_c, 1)
    multiply(at_c, 1)
    landed(0, at_x, 0)
    ship(4, land(at_x, 0), at_x, 0, at_y)
    ship(8, land(at_x, 0), at_x, 0, at_c)
    landed(3, at_y, 1)
    ship(5, land(at_y, 1), at_y, 1, at_x)
    ship(11, land(at_y, 1), at_y, 1, at_c)
    multiply(at_x, 0)
    multiply(at_y, 1)
    landed(8, c_x, 0)
    multiply(c_x, 0)
    landed(11, c_y, 1)
    multiply(c_y, 1)
    landed(1, at_x, 1)
    ship(9, land(at_x, 1), at_x, 1, at_c)
    landed(2, at_y, 0)
    ship(10, land(at_y, 0), at_y, 0, at_c)
    multiply(at_x, 1)
    multiply(at_y, 0)
    landed(9, c_x, 1)
    multiply(c_x, 1)
    landed(10, c_y, 0)
    multiply(c_y, 0)
    landed(4, at_d, 0)
    ship(12, land(at_d, 0), at_d, 0, at_c)
    landed(5, at_d, 1)
    ship(13, land(at_d, 1), at_d, 1, at_c)
    multiply(at_d, 0)
    multiply(at_d, 1)
    landed(12, c_d, 0)
    multiply(c_d, 0)
    landed(13, c_d, 1)
    multiply(c_d, 1)
    keep = pltpu.make_async_copy(wts, wfull_hbm, local_sem.at[3])
    keep.start()

    out_copies = []
    mine = pl.ds(pl.multiple_of(me * blk, blk), blk)
    for d in [*range(1, n), 0]:
        to = (me + d) % n

        @pl.loop(0, blk // 16)
        def _(t):
            picked = jnp.zeros((16, 2 * width), jnp.float32)
            for b in range(rows // blk):
                row = routes_ref[to, b : b + 1, :]
                wide = jnp.concatenate([row] * (2 * width // BLK), axis=1) > 0.5
                part = acc[pl.ds(pl.multiple_of(b * blk + t * 16, 16), 16), :]
                picked = jnp.where(wide, part, picked)
            outbound[to, pl.ds(pl.multiple_of(t * 16, 16), 16), :] = picked.astype(jnp.bfloat16)

        if d == 0:
            arrived[mine, :] = outbound[to]
            continue
        copy = pltpu.make_async_remote_copy(
            src_ref=outbound.at[to],
            dst_ref=arrived.at[mine, :],
            send_sem=out_send.at[d],
            recv_sem=out_recv.at[d],
            device_id={"dp": to},
            device_id_type=MESH,
        )
        copy.start()
        out_copies.append(copy)

    token_doc = token_doc_ref[:, 0:1]
    for copy in tag_copies:
        copy.wait()
    for copy in out_copies:
        copy.wait()
    tag_row = jnp.concatenate([arrived_tags[s, 0:1, :] for s in range(slots)], axis=1)
    live = tag_row == token_doc
    present = jnp.max(jnp.where(live, 1.0, 0.0), axis=1, keepdims=True) > 0.0
    scaling = HD ** (-0.5)
    back_copies = []
    for h in range(width // HD):
        hk, hv = pl.ds(h * HD, HD), pl.ds(width + h * HD, HD)
        q, g = q_ref[:, hk], g_ref[:, hk]
        scores = contract(q, arrived[:, hk], 1, 1) * scaling
        highest = jnp.max(jnp.where(live, scores, masked_value), axis=1, keepdims=True)
        highest = jnp.where(present, highest, 0.0)
        raised = jnp.exp(jnp.where(live, scores - highest, masked_value))
        totals = jnp.maximum(jnp.sum(raised, axis=1, keepdims=True), 1.0)
        attention = raised / totals
        rounded = attention.astype(jnp.bfloat16)
        grad_raw = contract(g, arrived[:, hv], 1, 1)
        deltas = jnp.sum(attention * grad_raw, axis=1, keepdims=True)
        score_grad = (attention * (grad_raw - deltas) * scaling).astype(jnp.bfloat16)
        grads[h, 0] = contract(score_grad, q, 0, 0).astype(jnp.bfloat16)
        grads[h, 1] = contract(rounded, g, 0, 0).astype(jnp.bfloat16)
        for d in range(1, n):
            to = (me + d) % n
            copy = pltpu.make_async_remote_copy(
                src_ref=grads.at[h, :, pl.ds(pl.multiple_of(to * blk, blk), blk), :],
                dst_ref=ret.at[h, :, pl.ds(pl.multiple_of(me * blk, blk), blk), :],
                send_sem=back_send.at[h, d],
                recv_sem=back_recv.at[h, d],
                device_id={"dp": to},
                device_id_type=MESH,
            )
            copy.start()
            back_copies.append(copy)
        ret[h, :, mine, :] = grads[h, :, mine, :]
        ctx_ref[:, hk] = jnp.dot(
            rounded, arrived[:, hv], preferred_element_type=jnp.float32
        ).astype(jnp.bfloat16)
        qg_ref[:, hk] = jnp.dot(
            score_grad, arrived[:, hk], preferred_element_type=jnp.float32
        ).astype(jnp.bfloat16)
    for copy in started:
        copy.wait_send()
    keep.wait()
    for copy in back_copies:
        copy.wait()
    put = pltpu.make_async_copy(ret, back_hbm, local_sem.at[0])
    put.start()
    put.wait()


def pick_kernel(bins_ref, back_ref, own_ref):
    heads = back_ref.shape[0]
    for h in range(heads):
        own_ref[:, pl.ds(h * HD, HD)] = back_ref[h, 0]
        own_ref[:, pl.ds((heads + h) * HD, HD)] = back_ref[h, 1]


def pick_blocks(back, bins):
    heads = back.shape[0]
    count = bins.shape[0]
    return pl.pallas_call(
        pick_kernel,
        out_shape=jax.ShapeDtypeStruct((count * BLK, 2 * heads * HD), back.dtype),
        grid_spec=pltpu.PrefetchScalarGridSpec(
            num_scalar_prefetch=1,
            grid=(count,),
            in_specs=[pl.BlockSpec((heads, 2, BLK, HD), lambda b, bins: (0, 0, bins[b], 0))],
            out_specs=pl.BlockSpec((BLK, 2 * heads * HD), lambda b, bins: (b, 0)),
        ),
    )(bins, back)


def front(n, queries, context_grad, encoder_rows, key_weight, value_weight, lengths, bins, docs):
    rows, model = encoder_rows.shape
    depth, width = key_weight.shape
    heads = width // HD
    tokens = queries.shape[0]
    hits = bins[:, None] == jnp.arange(n, dtype=jnp.int32)[None, :]
    slot_docs = jnp.sum(jnp.where(hits, docs[:, None] + 1, 0), axis=0) - 1
    tags = jnp.broadcast_to(slot_docs.astype(jnp.float32)[:, None, None], (n, 8, BLK))
    padded = jnp.pad(hits.astype(jnp.float32).T, ((0, 0), (0, -bins.shape[0] % 8)))
    routes = jnp.broadcast_to(padded[:, :, None], (n, padded.shape[1], BLK))
    position = lax.broadcasted_iota(jnp.int32, (tokens, BLK), 0)
    token_doc = jnp.zeros((tokens, BLK), jnp.float32)
    end = jnp.int32(0)
    for k in range(lengths.shape[1]):
        end = end + lengths[0, k]
        token_doc = token_doc + jnp.where(position >= end, 1.0, 0.0)
    vmem = pl.BlockSpec(memory_space=pltpu.VMEM)
    hbm = pl.BlockSpec(memory_space=pl.ANY)
    bf16 = jnp.bfloat16
    dma = pltpu.SemaphoreType.DMA
    return pl.pallas_call(
        functools.partial(front_kernel, n),
        out_shape=(
            jax.ShapeDtypeStruct((tokens, width), bf16),
            jax.ShapeDtypeStruct((tokens, width), bf16),
            jax.ShapeDtypeStruct((heads, 2, n * BLK, HD), bf16),
            jax.ShapeDtypeStruct((n, depth, 2 * width), bf16),
        ),
        in_specs=[vmem, vmem, hbm, vmem, vmem, vmem, vmem, vmem],
        out_specs=(vmem, vmem, hbm, hbm),
        scratch_shapes=[
            pltpu.VMEM((rows, model), bf16),
            pltpu.VMEM((n, depth, 2 * width), bf16),
            pltpu.VMEM((rows, 2 * width), jnp.float32),
            pltpu.VMEM((n, BLK, 2 * width), bf16),
            pltpu.VMEM((n * BLK, 2 * width), bf16),
            pltpu.VMEM((n, 8, BLK), jnp.float32),
            pltpu.VMEM((heads, 2, n * BLK, HD), bf16),
            pltpu.VMEM((heads, 2, n * BLK, HD), bf16),
            dma((4,)),
            dma((14,)),
            dma((14,)),
            dma((n,)),
            dma((n,)),
            dma((n,)),
            dma((n,)),
            dma((heads, n)),
            dma((heads, n)),
        ],
        compiler_params=pltpu.CompilerParams(
            collective_id=0, has_side_effects=True, vmem_limit_bytes=62 * 1024 * 1024
        ),
    )(
        queries,
        context_grad,
        encoder_rows,
        key_weight,
        value_weight,
        tags,
        routes,
        token_doc,
    )


def line_sum(part_of, count):
    z = lax.axis_index("mp")
    total = part_of(z)
    for direction in (1, -1):
        carried = None
        for step in range(count - 1):
            if direction == 1:
                dest = jnp.clip(z + count - 1 - step, 0, count - 1)
                pairs = [(k, k + 1) for k in range(count - 1) if k <= step]
            else:
                dest = jnp.clip(z - (count - 1) + step, 0, count - 1)
                pairs = [(k, k - 1) for k in range(1, count) if count - 1 - k <= step]
            term = part_of(dest)
            if carried is not None:
                term = term + carried.astype(jnp.float32)
            carried = lax.ppermute(term.astype(jnp.bfloat16), "mp", pairs)
        total = total + carried.astype(jnp.float32)
    return total.astype(jnp.bfloat16)


def per_device_cube(
    queries,
    context_grad,
    encoder_rows,
    key_weight,
    value_weight,
    document_lengths,
    block_bin,
    block_document,
):
    n, count = lax.axis_size("dp"), lax.axis_size("mp")
    width = key_weight.shape[1]
    context, query_grad, back, weights = front(
        n,
        queries,
        context_grad,
        encoder_rows,
        key_weight,
        value_weight,
        document_lengths,
        block_bin,
        block_document,
    )
    weights = weights.reshape(-1, 2 * width)
    own = pick_blocks(back, block_bin)
    out_width = weights.shape[0] // count
    weight_terms = contract(encoder_rows, own, 0, 0)
    weight_sums = lax.psum_scatter(
        weight_terms.astype(jnp.bfloat16), "dp", scatter_dimension=0, tiled=True
    )

    def part_of(dest):
        piece = lax.dynamic_slice_in_dim(weights, dest * out_width, out_width, 0)
        return contract(own, piece, 1, 1)

    encoder_grad = line_sum(part_of, count)
    return context, query_grad, encoder_grad, weight_sums[:, :width], weight_sums[:, width:]


def solution(mesh):
    in_specs = (
        P("dp", "mp"),
        P("dp", "mp"),
        P("dp", None),
        P("dp", "mp"),
        P("dp", "mp"),
        P("dp", None),
        P("dp"),
        P("dp"),
    )
    out_specs = (P("dp", "mp"), P("dp", "mp"), P("dp", "mp"), P("dp", "mp"), P("dp", "mp"))
    cube = mesh.shape["dp"] == 2 * 2 * 2
    return jax.shard_map(
        per_device_cube if cube else per_device, mesh=mesh, in_specs=in_specs, out_specs=out_specs, check_vma=False
    )
```

```python
import functools

import jax
import jax.numpy as jnp
from jax import lax
from jax.experimental import pallas as pl
from jax.experimental.pallas import tpu as pltpu
from jax.sharding import PartitionSpec as P

HD = 256
BLK = 128


masked_value = -1e30


def attend_weights(scores, live_mask):
    present = jnp.any(live_mask, axis=1)[None, :, None]
    blocked = jnp.where(live_mask[None], scores, masked_value)
    highest = jnp.max(blocked, axis=2, keepdims=True)
    highest = jnp.where(present, highest, 0.0)
    raised = jnp.exp(jnp.where(live_mask[None], scores - highest, masked_value))
    totals = jnp.maximum(jnp.sum(raised, axis=2, keepdims=True), 1.0)
    return raised / totals


def token_documents(lengths, token_count):
    doc_ends = jnp.cumsum(lengths)
    positions = jnp.arange(token_count, dtype=jnp.int32)
    return jnp.sum((doc_ends[None, :] <= positions[:, None]).astype(jnp.int32), axis=1)


def per_device(
    queries,
    context_grad,
    encoder_rows,
    key_weight,
    value_weight,
    document_lengths,
    block_bin,
    block_document,
):
    bin_count = lax.axis_size("dp")
    full_key, full_value = (
        lax.all_gather(key_weight, "dp", axis=0, tiled=True),
        lax.all_gather(value_weight, "dp", axis=0, tiled=True),
    )
    head_width = full_key.shape[1]
    head_count = head_width // HD
    block_rows = BLK
    blocks_here = block_bin.shape[0]
    both_weights = jnp.concatenate([full_key, full_value], axis=1)
    projected = jnp.dot(encoder_rows, both_weights, preferred_element_type=jnp.float32).astype(
        jnp.bfloat16
    )
    route_table = (block_bin[:, None] == jnp.arange(bin_count, dtype=jnp.int32)[None, :]).astype(
        jnp.bfloat16
    )
    flat_blocks = projected.reshape(blocks_here, block_rows * 2 * head_width)
    outbound = lax.dot_general(
        route_table, flat_blocks, (((0,), (0,)), ((), ())), preferred_element_type=jnp.float32
    )
    outbound = outbound.astype(jnp.bfloat16).reshape(bin_count, block_rows, 2 * head_width)
    slot_docs = (
        lax.dot_general(
            route_table.astype(jnp.float32),
            (block_document + 1).astype(jnp.float32),
            (((0,), (0,)), ((), ())),
        )
        - 1.0
    )
    tag_rows = jnp.broadcast_to(slot_docs[:, None], (bin_count, block_rows)).astype(jnp.bfloat16)
    arrived, arrived_tags = (
        lax.all_to_all(outbound, "dp", split_axis=0, concat_axis=0, tiled=True),
        lax.all_to_all(tag_rows, "dp", split_axis=0, concat_axis=0, tiled=True),
    )
    key_slots = arrived[:, :, :head_width].reshape(bin_count * block_rows, head_count, HD)
    value_slots = arrived[:, :, head_width:].reshape(bin_count * block_rows, head_count, HD)
    token_count = queries.shape[0]
    token_docs = token_documents(document_lengths[0], token_count).astype(jnp.float32)
    live_mask = arrived_tags.reshape(-1).astype(jnp.float32)[None, :] == token_docs[:, None]
    query_heads = queries.reshape(token_count, head_count, HD)
    grad_heads = context_grad.reshape(token_count, head_count, HD)
    scaling = HD ** (-0.5)
    scores = (
        jnp.einsum("thd,shd->hts", query_heads, key_slots, preferred_element_type=jnp.float32)
        * scaling
    )
    attention = attend_weights(scores, live_mask)
    rounded = attention.astype(jnp.bfloat16)
    context = jnp.einsum(
        "hts,shd->thd", rounded, value_slots, preferred_element_type=jnp.float32
    ).astype(jnp.bfloat16)
    grad_raw = jnp.einsum(
        "thd,shd->hts", grad_heads, value_slots, preferred_element_type=jnp.float32
    )
    deltas = jnp.sum(attention * grad_raw, axis=2, keepdims=True)
    score_grad = (attention * (grad_raw - deltas) * scaling).astype(jnp.bfloat16)
    query_grad = jnp.einsum(
        "hts,shd->thd", score_grad, key_slots, preferred_element_type=jnp.float32
    ).astype(jnp.bfloat16)
    key_grad = jnp.einsum(
        "hts,thd->shd", score_grad, query_heads, preferred_element_type=jnp.float32
    ).astype(jnp.bfloat16)
    value_grad = jnp.einsum(
        "hts,thd->shd", rounded, grad_heads, preferred_element_type=jnp.float32
    ).astype(jnp.bfloat16)
    slot_grads = jnp.concatenate(
        [
            key_grad.reshape(bin_count, block_rows, head_width),
            value_grad.reshape(bin_count, block_rows, head_width),
        ],
        axis=2,
    )
    returned = lax.all_to_all(slot_grads, "dp", split_axis=0, concat_axis=0, tiled=True)
    own_grads = jnp.dot(
        route_table,
        returned.reshape(bin_count, block_rows * 2 * head_width),
        preferred_element_type=jnp.float32,
    )
    own_grads = own_grads.astype(jnp.bfloat16).reshape(encoder_rows.shape[0], 2 * head_width)
    weight_terms = lax.dot_general(
        encoder_rows, own_grads, (((0,), (0,)), ((), ())), preferred_element_type=jnp.float32
    )
    weight_sums = lax.psum_scatter(
        weight_terms.astype(jnp.bfloat16), "dp", scatter_dimension=0, tiled=True
    ).astype(jnp.float32)
    key_weight_grad = weight_sums[:, :head_width].astype(jnp.bfloat16)
    value_weight_grad = weight_sums[:, head_width:].astype(jnp.bfloat16)
    row_terms = lax.dot_general(
        own_grads, both_weights, (((1,), (1,)), ((), ())), preferred_element_type=jnp.float32
    )
    encoder_grad = lax.psum_scatter(
        row_terms.astype(jnp.bfloat16), "mp", scatter_dimension=1, tiled=True
    )
    return (
        context.reshape(token_count, head_width),
        query_grad.reshape(token_count, head_width),
        encoder_grad,
        key_weight_grad,
        value_weight_grad,
    )


MESH = pl.DeviceIdType.MESH


def contract(a, b, dim_a, dim_b):
    return lax.dot_general(
        a, b, (((dim_a,), (dim_b,)), ((), ())), preferred_element_type=jnp.float32
    )


def front_kernel(
    n,
    q_ref,
    g_ref,
    enc_hbm,
    kw_ref,
    vw_ref,
    tags_ref,
    routes_ref,
    token_doc_ref,
    ctx_ref,
    qg_ref,
    back_hbm,
    wfull_hbm,
    enc,
    wts,
    acc,
    outbound,
    arrived,
    arrived_tags,
    grads,
    ret,
    local_sem,
    gather_send,
    gather_recv,
    tag_send,
    tag_recv,
    out_send,
    out_recv,
    back_send,
    back_recv,
):
    me = lax.axis_index("dp")
    core = me % 2
    x = (me // 2) % 2
    y = me // 4

    def place(py, px, pc):
        return (py * 2 + px) * 2 + pc

    at_x, at_y = place(y, 1 - x, core), place(1 - y, x, core)
    at_c, at_d = place(y, x, 1 - core), place(1 - y, 1 - x, core)
    c_x, c_y = place(y, 1 - x, 1 - core), place(1 - y, x, 1 - core)
    c_d = place(1 - y, 1 - x, 1 - core)
    depth, width = kw_ref.shape
    rows = enc.shape[0]
    slots = n
    blk = BLK

    load_enc = pltpu.make_async_copy(enc_hbm, enc, local_sem.at[0])
    load_enc.start()
    barrier = pltpu.get_barrier_semaphore()
    for d in range(1, n):
        pl.semaphore_signal(
            barrier, inc=1, device_id={"dp": (me + d) % n}, device_id_type=MESH
        )
    pl.semaphore_wait(barrier, n - 1)

    def land(src, part):
        return wts.at[src, :, pl.ds(part * width, width)]

    started = []

    def ship(ident, ref, src, part, to):
        copy = pltpu.make_async_remote_copy(
            src_ref=ref,
            dst_ref=land(src, part),
            send_sem=gather_send.at[ident],
            recv_sem=gather_recv.at[ident],
            device_id={"dp": to},
            device_id_type=MESH,
        )
        copy.start()
        started.append(copy)

    def landed(ident, src, part):
        pltpu.make_async_remote_copy(
            src_ref=land(src, part),
            dst_ref=land(src, part),
            send_sem=gather_send.at[ident],
            recv_sem=gather_recv.at[ident],
            device_id={"dp": at_c},
            device_id_type=MESH,
        ).wait_recv()

    ship(0, kw_ref, me, 0, at_x)
    ship(3, vw_ref, me, 1, at_y)
    ship(1, vw_ref, me, 1, at_x)
    ship(2, kw_ref, me, 0, at_y)
    ship(6, kw_ref, me, 0, at_c)
    ship(7, vw_ref, me, 1, at_c)
    own_k = pltpu.make_async_copy(kw_ref, land(me, 0), local_sem.at[1])
    own_v = pltpu.make_async_copy(vw_ref, land(me, 1), local_sem.at[2])
    own_k.start()
    own_v.start()
    tag_copies = []
    for d in range(1, n):
        to = (me + d) % n
        copy = pltpu.make_async_remote_copy(
            src_ref=tags_ref.at[to],
            dst_ref=arrived_tags.at[me],
            send_sem=tag_send.at[d],
            recv_sem=tag_recv.at[d],
            device_id={"dp": to},
            device_id_type=MESH,
        )
        copy.start()
        tag_copies.append(copy)
    arrived_tags[me] = tags_ref[me]
    own_k.wait()
    own_v.wait()
    load_enc.wait()

    tile = rows // 2

    def multiply(src, part, first=False):
        columns = pl.ds(pl.multiple_of(src * depth, depth), depth)
        cols = pl.ds(part * width, width)

        @pl.loop(0, 2)
        def _(t):
            r = pl.ds(pl.multiple_of(t * tile, tile), tile)
            product = jnp.dot(
                enc[r, columns], wts[src, :, cols], preferred_element_type=jnp.float32
            )
            if first:
                acc[r, cols] = product
            else:
                acc[r, cols] += product

    multiply(me, 0, True)
    multiply(me, 1, True)
    landed(6, at_c, 0)
    multiply(at_c, 0)
    landed(7, at_c, 1)
    multiply(at_c, 1)
    landed(0, at_x, 0)
    ship(4, land(at_x, 0), at_x, 0, at_y)
    ship(8, land(at_x, 0), at_x, 0, at_c)
    landed(3, at_y, 1)
    ship(5, land(at_y, 1), at_y, 1, at_x)
    ship(11, land(at_y, 1), at_y, 1, at_c)
    multiply(at_x, 0)
    multiply(at_y, 1)
    landed(8, c_x, 0)
    multiply(c_x, 0)
    landed(11, c_y, 1)
    multiply(c_y, 1)
    landed(1, at_x, 1)
    ship(9, land(at_x, 1), at_x, 1, at_c)
    landed(2, at_y, 0)
    ship(10, land(at_y, 0), at_y, 0, at_c)
    multiply(at_x, 1)
    multiply(at_y, 0)
    landed(9, c_x, 1)
    multiply(c_x, 1)
    landed(10, c_y, 0)
    multiply(c_y, 0)
    landed(4, at_d, 0)
    ship(12, land(at_d, 0), at_d, 0, at_c)
    landed(5, at_d, 1)
    ship(13, land(at_d, 1), at_d, 1, at_c)
    multiply(at_d, 0)
    multiply(at_d, 1)
    landed(12, c_d, 0)
    multiply(c_d, 0)
    landed(13, c_d, 1)
    multiply(c_d, 1)
    keep = pltpu.make_async_copy(wts, wfull_hbm, local_sem.at[3])
    keep.start()

    out_copies = []
    mine = pl.ds(pl.multiple_of(me * blk, blk), blk)
    for d in [*range(1, n), 0]:
        to = (me + d) % n

        @pl.loop(0, blk // 16)
        def _(t):
            picked = jnp.zeros((16, 2 * width), jnp.float32)
            for b in range(rows // blk):
                row = routes_ref[to, b : b + 1, :]
                wide = jnp.concatenate([row] * (2 * width // BLK), axis=1) > 0.5
                part = acc[pl.ds(pl.multiple_of(b * blk + t * 16, 16), 16), :]
                picked = jnp.where(wide, part, picked)
            outbound[to, pl.ds(pl.multiple_of(t * 16, 16), 16), :] = picked.astype(jnp.bfloat16)

        if d == 0:
            arrived[mine, :] = outbound[to]
            continue
        copy = pltpu.make_async_remote_copy(
            src_ref=outbound.at[to],
            dst_ref=arrived.at[mine, :],
            send_sem=out_send.at[d],
            recv_sem=out_recv.at[d],
            device_id={"dp": to},
            device_id_type=MESH,
        )
        copy.start()
        out_copies.append(copy)

    token_doc = token_doc_ref[:, 0:1]
    for copy in tag_copies:
        copy.wait()
    for copy in out_copies:
        copy.wait()
    tag_row = jnp.concatenate([arrived_tags[s, 0:1, :] for s in range(slots)], axis=1)
    live = tag_row == token_doc
    present = jnp.max(jnp.where(live, 1.0, 0.0), axis=1, keepdims=True) > 0.0
    scaling = HD ** (-0.5)
    back_copies = []
    for h in range(width // HD):
        hk, hv = pl.ds(h * HD, HD), pl.ds(width + h * HD, HD)
        q, g = q_ref[:, hk], g_ref[:, hk]
        scores = contract(q, arrived[:, hk], 1, 1) * scaling
        highest = jnp.max(jnp.where(live, scores, masked_value), axis=1, keepdims=True)
        highest = jnp.where(present, highest, 0.0)
        raised = jnp.exp(jnp.where(live, scores - highest, masked_value))
        totals = jnp.maximum(jnp.sum(raised, axis=1, keepdims=True), 1.0)
        attention = raised / totals
        rounded = attention.astype(jnp.bfloat16)
        grad_raw = contract(g, arrived[:, hv], 1, 1)
        deltas = jnp.sum(attention * grad_raw, axis=1, keepdims=True)
        score_grad = (attention * (grad_raw - deltas) * scaling).astype(jnp.bfloat16)
        grads[h, 0] = contract(score_grad, q, 0, 0).astype(jnp.bfloat16)
        grads[h, 1] = contract(rounded, g, 0, 0).astype(jnp.bfloat16)
        for d in range(1, n):
            to = (me + d) % n
            copy = pltpu.make_async_remote_copy(
                src_ref=grads.at[h, :, pl.ds(pl.multiple_of(to * blk, blk), blk), :],
                dst_ref=ret.at[h, :, pl.ds(pl.multiple_of(me * blk, blk), blk), :],
                send_sem=back_send.at[h, d],
                recv_sem=back_recv.at[h, d],
                device_id={"dp": to},
                device_id_type=MESH,
            )
            copy.start()
            back_copies.append(copy)
        ret[h, :, mine, :] = grads[h, :, mine, :]
        ctx_ref[:, hk] = jnp.dot(
            rounded, arrived[:, hv], preferred_element_type=jnp.float32
        ).astype(jnp.bfloat16)
        qg_ref[:, hk] = jnp.dot(
            score_grad, arrived[:, hk], preferred_element_type=jnp.float32
        ).astype(jnp.bfloat16)
    for copy in started:
        copy.wait_send()
    keep.wait()
    for copy in back_copies:
        copy.wait()
    put = pltpu.make_async_copy(ret, back_hbm, local_sem.at[0])
    put.start()
    put.wait()


def pick_kernel(bins_ref, back_ref, own_ref):
    heads = back_ref.shape[0]
    for h in range(heads):
        own_ref[:, pl.ds(h * HD, HD)] = back_ref[h, 0]
        own_ref[:, pl.ds((heads + h) * HD, HD)] = back_ref[h, 1]


def pick_blocks(back, bins):
    heads = back.shape[0]
    count = bins.shape[0]
    return pl.pallas_call(
        pick_kernel,
        out_shape=jax.ShapeDtypeStruct((count * BLK, 2 * heads * HD), back.dtype),
        grid_spec=pltpu.PrefetchScalarGridSpec(
            num_scalar_prefetch=1,
            grid=(count,),
            in_specs=[pl.BlockSpec((heads, 2, BLK, HD), lambda b, bins: (0, 0, bins[b], 0))],
            out_specs=pl.BlockSpec((BLK, 2 * heads * HD), lambda b, bins: (b, 0)),
        ),
    )(bins, back)


def front(n, queries, context_grad, encoder_rows, key_weight, value_weight, lengths, bins, docs):
    rows, model = encoder_rows.shape
    depth, width = key_weight.shape
    heads = width // HD
    tokens = queries.shape[0]
    hits = bins[:, None] == jnp.arange(n, dtype=jnp.int32)[None, :]
    slot_docs = jnp.sum(jnp.where(hits, docs[:, None] + 1, 0), axis=0) - 1
    tags = jnp.broadcast_to(slot_docs.astype(jnp.float32)[:, None, None], (n, 8, BLK))
    padded = jnp.pad(hits.astype(jnp.float32).T, ((0, 0), (0, -bins.shape[0] % 8)))
    routes = jnp.broadcast_to(padded[:, :, None], (n, padded.shape[1], BLK))
    position = lax.broadcasted_iota(jnp.int32, (tokens, BLK), 0)
    token_doc = jnp.zeros((tokens, BLK), jnp.float32)
    end = jnp.int32(0)
    for k in range(lengths.shape[1]):
        end = end + lengths[0, k]
        token_doc = token_doc + jnp.where(position >= end, 1.0, 0.0)
    vmem = pl.BlockSpec(memory_space=pltpu.VMEM)
    hbm = pl.BlockSpec(memory_space=pl.ANY)
    bf16 = jnp.bfloat16
    dma = pltpu.SemaphoreType.DMA
    return pl.pallas_call(
        functools.partial(front_kernel, n),
        out_shape=(
            jax.ShapeDtypeStruct((tokens, width), bf16),
            jax.ShapeDtypeStruct((tokens, width), bf16),
            jax.ShapeDtypeStruct((heads, 2, n * BLK, HD), bf16),
            jax.ShapeDtypeStruct((n, depth, 2 * width), bf16),
        ),
        in_specs=[vmem, vmem, hbm, vmem, vmem, vmem, vmem, vmem],
        out_specs=(vmem, vmem, hbm, hbm),
        scratch_shapes=[
            pltpu.VMEM((rows, model), bf16),
            pltpu.VMEM((n, depth, 2 * width), bf16),
            pltpu.VMEM((rows, 2 * width), jnp.float32),
            pltpu.VMEM((n, BLK, 2 * width), bf16),
            pltpu.VMEM((n * BLK, 2 * width), bf16),
            pltpu.VMEM((n, 8, BLK), jnp.float32),
            pltpu.VMEM((heads, 2, n * BLK, HD), bf16),
            pltpu.VMEM((heads, 2, n * BLK, HD), bf16),
            dma((4,)),
            dma((14,)),
            dma((14,)),
            dma((n,)),
            dma((n,)),
            dma((n,)),
            dma((n,)),
            dma((heads, n)),
            dma((heads, n)),
        ],
        compiler_params=pltpu.CompilerParams(
            collective_id=0, has_side_effects=True, vmem_limit_bytes=62 * 1024 * 1024
        ),
    )(
        queries,
        context_grad,
        encoder_rows,
        key_weight,
        value_weight,
        tags,
        routes,
        token_doc,
    )


def line_kernel(
    count, own_ref, weights_hbm, out_ref, weights, got, sent, total, load_sem, send_sem, recv_sem
):
    z = lax.axis_index("mp")
    chunks = own_ref.shape[0] // BLK
    right, left = (z + 1) % count, (z + count - 1) % count
    loads = [
        pltpu.make_async_copy(weights_hbm.at[d], weights.at[d], load_sem.at[d])
        for d in range(count)
    ]
    for load in loads:
        load.start()
    barrier = pltpu.get_barrier_semaphore()
    for d in range(1, count):
        pl.semaphore_signal(
            barrier, inc=1, device_id={"mp": (z + d) % count}, device_id_type=MESH
        )
    pl.semaphore_wait(barrier, count - 1)
    for load in loads:
        load.wait()

    def link(way, dest, r):
        return pltpu.make_async_remote_copy(
            src_ref=sent.at[way, dest, r],
            dst_ref=got.at[way, dest, r],
            send_sem=send_sem.at[way, dest, r],
            recv_sem=recv_sem.at[way, dest, r],
            device_id={"mp": left if way else right},
            device_id_type=MESH,
        )

    def rows(r):
        return pl.ds(pl.multiple_of(r * BLK, BLK), BLK)

    def pass_on(way, dest, r):
        first = z == (count - 1 if way else 0)
        total[...] = contract(own_ref[rows(r), :], weights[dest], 1, 1)

        @pl.when(first)
        def _():
            sent[way, dest, r] = total[...].astype(jnp.bfloat16)

        @pl.when(jnp.logical_not(first))
        def _():
            link(way, dest, r).wait_recv()
            added = total[...] + got[way, dest, r].astype(jnp.float32)
            sent[way, dest, r] = added.astype(jnp.bfloat16)

        link(way, dest, r).start()

    for phase in range(count - 1):

        @pl.loop(0, chunks)
        def _(r):
            @pl.when(z < count - 1 - phase)
            def _():
                pass_on(0, count - 1 - phase, r)

            @pl.when(z > phase)
            def _():
                pass_on(1, phase, r)

    @pl.loop(0, chunks)
    def _(r):
        total[...] = contract(own_ref[rows(r), :], weights[z], 1, 1)

        @pl.when(z > 0)
        def _():
            link(0, z, r).wait_recv()
            total[...] += got[0, z, r].astype(jnp.float32)

        @pl.when(z < count - 1)
        def _():
            link(1, z, r).wait_recv()
            total[...] += got[1, z, r].astype(jnp.float32)

        out_ref[rows(r), :] = total[...].astype(jnp.bfloat16)

    for phase in range(count - 1):

        @pl.loop(0, chunks)
        def _(r):
            @pl.when(z < count - 1 - phase)
            def _():
                link(0, count - 1 - phase, r).wait_send()

            @pl.when(z > phase)
            def _():
                link(1, phase, r).wait_send()


def line_sum(own, weights, count):
    rows, width = own.shape
    out_width = weights.shape[0] // count
    chunks = rows // BLK
    vmem = pl.BlockSpec(memory_space=pltpu.VMEM)
    dma = pltpu.SemaphoreType.DMA
    return pl.pallas_call(
        functools.partial(line_kernel, count),
        out_shape=jax.ShapeDtypeStruct((rows, out_width), own.dtype),
        in_specs=[vmem, pl.BlockSpec(memory_space=pl.ANY)],
        out_specs=vmem,
        scratch_shapes=[
            pltpu.VMEM((count, out_width, width), own.dtype),
            pltpu.VMEM((2, count, chunks, BLK, out_width), own.dtype),
            pltpu.VMEM((2, count, chunks, BLK, out_width), own.dtype),
            pltpu.VMEM((BLK, out_width), jnp.float32),
            dma((count,)),
            dma((2, count, chunks)),
            dma((2, count, chunks)),
        ],
        compiler_params=pltpu.CompilerParams(
            collective_id=1, has_side_effects=True, vmem_limit_bytes=58 * 1024 * 1024
        ),
        cost_estimate=pl.CostEstimate(
            flops=2 * rows * width * out_width * count,
            bytes_accessed=300 * 1024 * 1024,
            transcendentals=0,
        ),
    )(own, weights.reshape(count, out_width, width))


def per_device_cube(
    queries,
    context_grad,
    encoder_rows,
    key_weight,
    value_weight,
    document_lengths,
    block_bin,
    block_document,
):
    n, count = lax.axis_size("dp"), lax.axis_size("mp")
    width = key_weight.shape[1]
    context, query_grad, back, weights = front(
        n,
        queries,
        context_grad,
        encoder_rows,
        key_weight,
        value_weight,
        document_lengths,
        block_bin,
        block_document,
    )
    weights = weights.reshape(-1, 2 * width)
    own = pick_blocks(back, block_bin)
    weight_terms = contract(encoder_rows, own, 0, 0)
    weight_sums = lax.psum_scatter(
        weight_terms.astype(jnp.bfloat16), "dp", scatter_dimension=0, tiled=True
    )
    encoder_grad = line_sum(own, weights, count)
    return context, query_grad, encoder_grad, weight_sums[:, :width], weight_sums[:, width:]


def solution(mesh):
    in_specs = (
        P("dp", "mp"),
        P("dp", "mp"),
        P("dp", None),
        P("dp", "mp"),
        P("dp", "mp"),
        P("dp", None),
        P("dp"),
        P("dp"),
    )
    out_specs = (P("dp", "mp"), P("dp", "mp"), P("dp", "mp"), P("dp", "mp"), P("dp", "mp"))
    cube = mesh.shape["dp"] == 2 * 2 * 2
    return jax.shard_map(
        per_device_cube if cube else per_device, mesh=mesh, in_specs=in_specs, out_specs=out_specs, check_vma=False
    )
```
